32 devices in a mesh: blk: 2 (over y), rep: 4 (over z), sub: 4 (over x, core).
Axes of the slice: x: 2, y: 2, z: 4, core: 2. Of those that a mesh axis runs over, the one named last changes fastest.
Arguments:
- image_embed: bfloat16 [2048, 1152], P(('blk', 'rep', 'sub')), may hold values from -60 to 60
- text_embed: bfloat16 [2048, 1152], P(('blk', 'rep', 'sub')), may hold values from -60 to 60
- image_ids: int32 [2048], P(('blk', 'rep', 'sub')), may hold values from 0 to 1023
- text_ids: int32 [2048], P(('blk', 'rep', 'sub')), may hold values from 0 to 1023
Outputs:
- image_grad: float32 [2048, 1152], P(('blk', 'rep', 'sub'))
- text_grad: float32 [2048, 1152], P(('blk', 'rep', 'sub'))
The draws below stay inside these ranges and needn't reach their ends.
All inputs are finite; a program needn't handle non-finite values.
Results may differ from the reference program's by a relative error of at most 0.008.
Values may be sent and summed in bfloat16 or wider, within the bound.
No kernel may reach another device: no remote copies, remote signals or barrier semaphores. Data moves between devices by JAX's collectives and lax.ppermute only.
A program may use at most 64 MiB of HBM per device.

```python
import math
import jax
import jax.numpy as jnp
from jax import lax

D = 1152
TOKENS = 2048


def rough_rows(key, salt):
    key = jax.random.fold_in(key, salt)
    first, second = jax.random.split(key, 2)
    base = jnp.clip(jax.random.normal(first, (TOKENS, D), jnp.float32), -6.0, 6.0)
    scale = jnp.exp(jax.random.uniform(second, (TOKENS, 1), jnp.float32) * math.log(10.0))
    return (base * scale).astype(jnp.bfloat16)


def draw_image_embed(key, part):
    return rough_rows(key, 11)


def draw_text_embed(key, part):
    return rough_rows(key, 23)


def set_ends(array, key, smallest, top_value):
    spot = [jax.random.randint(jax.random.fold_in(key, axis), (), 0, length) for axis, length in enumerate(array.shape)]
    widest = array.shape.index(max(array.shape))
    next_to = spot[:widest] + [(spot[widest] + 1) % array.shape[widest]] + spot[widest + 1:]
    return array.at[tuple(spot)].set(smallest).at[tuple(next_to)].set(top_value)


def setup_inputs(seed: int = 0) -> dict:
    seeds = jax.random.split(jax.random.key(seed), 5)
    return {
        "image_embed": draw_image_embed(jax.random.fold_in(seeds[4], 71), 0),
        "text_embed": draw_text_embed(jax.random.fold_in(seeds[4], 71), 0),
        "image_ids": set_ends(jax.random.randint(seeds[2], (TOKENS,), 0, TOKENS // 2), jax.random.fold_in(seeds[2], 1), 0, (TOKENS // 2) - 1).astype(jnp.int32),
        "text_ids": set_ends(jax.random.randint(seeds[3], (TOKENS,), 0, TOKENS // 2), jax.random.fold_in(seeds[3], 1), 0, (TOKENS // 2) - 1).astype(jnp.int32),
    }


logit_scale = 30.0
logit_bias = -3.0

def unit_rows(embed):
    values = embed.astype(jnp.float32)
    inverse = lax.rsqrt(lax.optimization_barrier(jnp.sum(values * values, axis=1, keepdims=True)) + 1e-06)
    return (values * inverse, inverse)

def project(unit, inverse, grad):
    along = lax.optimization_barrier(jnp.sum(unit * grad, axis=1, keepdims=True))
    return (grad - unit * along) * inverse

def reference(image_embed, text_embed, image_ids, text_ids):
    img_unit, img_inv = unit_rows(image_embed)
    txt_unit, txt_inv = unit_rows(text_embed)
    img_half = img_unit.astype(jnp.bfloat16)
    text_subset = txt_unit.astype(jnp.bfloat16)
    block = math.gcd(TOKENS, 1024)
    img_blocks = img_half.reshape(TOKENS // block, block, D)
    id_blocks = image_ids.reshape(TOKENS // block, block)

    def step(carry, item):
        batch_rows, keys = item
        pair_logits = logit_scale * jnp.dot(batch_rows, text_subset.T, preferred_element_type=jnp.float32) + logit_bias
        label_sign = (keys[:, None] == text_ids[None, :]).astype(jnp.float32)
        gradient_factor = (logit_scale * (jax.nn.sigmoid(pair_logits) - label_sign)).astype(jnp.bfloat16)
        grad_rows = jnp.dot(gradient_factor, text_subset, preferred_element_type=jnp.float32)
        carry = carry + lax.dot_general(gradient_factor, batch_rows, (((0,), (0,)), ((), ())), preferred_element_type=jnp.float32)
        return (carry, grad_rows)
    start = jnp.zeros((TOKENS, D), jnp.float32)
    g_txt, g_img = lax.scan(step, start, (img_blocks, id_blocks))
    g_img = g_img.reshape(TOKENS, D)
    return (project(img_unit, img_inv, g_img), project(txt_unit, txt_inv, g_txt))
```

```python
import jax
import jax.numpy as jnp
from jax import lax
from jax.experimental import pallas as pl
from jax.experimental.pallas import tpu as pltpu
from jax.sharding import PartitionSpec as P

logit_scale = 30.0
logit_bias = -3.0
LANES = 128
ID_BITS = 32

NT = (((1,), (1,)), ((), ()))
NN = (((1,), (0,)), ((), ()))
TN = (((0,), (0,)), ((), ()))
VMEM = pl.BlockSpec(memory_space=pltpu.VMEM)


def dot(a, b, dims):
    return lax.dot_general(a, b, dims, preferred_element_type=jnp.float32)


def pack_kernel(img_ref, txt_ref, img_id_ref, txt_id_ref, img_out, txt_out):
    for embed, ids, out in ((img_ref, img_id_ref, img_out), (txt_ref, txt_id_ref, txt_out)):
        rows, width = embed.shape
        values = embed[...].astype(jnp.float32)
        inverse = lax.rsqrt(jnp.sum(values * values, axis=1, keepdims=True) + 1e-06)
        out[:, :width] = (values * inverse).astype(jnp.bfloat16)
        place = lax.broadcasted_iota(jnp.int32, (LANES, rows), 0)
        bit = lax.shift_right_logical(jnp.broadcast_to(ids[...], (LANES, rows)), place & (ID_BITS - 1)) & 1
        sign = jnp.where(place < ID_BITS, (2 * bit - 1).astype(jnp.float32), 0.0)
        eye = (lax.broadcasted_iota(jnp.int32, (rows, rows), 0) == lax.broadcasted_iota(jnp.int32, (rows, rows), 1))
        eye = jnp.where(eye, 1.0, 0.0).astype(jnp.bfloat16)
        out[:, width:] = dot(eye, sign.astype(jnp.bfloat16), NT).astype(jnp.bfloat16)


def pack(image_embed, text_embed, image_ids, text_ids):
    rows, width = image_embed.shape
    out = jax.ShapeDtypeStruct((rows, width + LANES), jnp.bfloat16)
    return pl.pallas_call(
        pack_kernel, out_shape=(out, out), in_specs=[VMEM] * 4, out_specs=(VMEM, VMEM), name="pack",
    )(image_embed, text_embed, image_ids.reshape(1, rows), text_ids.reshape(1, rows))


def pair_kernel(n_img, n_txt, width, *refs):
    img_refs, txt_refs = refs[:n_img], refs[n_img : n_img + n_txt]
    img_out = refs[n_img + n_txt : 2 * n_img + n_txt]
    keep_out, swap_out, images, texts = refs[2 * n_img + n_txt :]
    rows = img_refs[0].shape[0]
    for k, ref in enumerate(img_refs):
        images[k * rows : (k + 1) * rows, :] = ref[...]
    for k, ref in enumerate(txt_refs):
        texts[k * rows : (k + 1) * rows, :] = ref[...]
    logits = logit_scale * dot(images[:, :width], texts[:, :width], NT) + logit_bias
    label = jnp.where(dot(images[:, width:], texts[:, width:], NT) == float(ID_BITS), 1.0, 0.0)
    factor = (logit_scale * (jax.nn.sigmoid(logits) - label)).astype(jnp.bfloat16)
    for k, out in enumerate(img_out):
        out[...] = dot(factor[k * rows : (k + 1) * rows, :], texts[:, :width], NN).astype(out.dtype)
    half = n_txt * rows // 2
    keep_out[...] = dot(factor[:, :half], images[:, :width], TN)
    swap_out[...] = dot(factor[:, half:], images[:, :width], TN).astype(swap_out.dtype)


def pair_terms(images, texts, width):
    rows, full = images[0].shape
    n_img, n_txt = len(images), len(texts)
    f32, b16 = jnp.float32, jnp.bfloat16
    shape = jax.ShapeDtypeStruct
    outs = [shape((rows, width), f32)] + [shape((rows, width), b16)] * (n_img - 1)
    outs += [shape((n_txt * rows // 2, width), f32), shape((n_txt * rows // 2, width), b16)]
    return pl.pallas_call(
        lambda *refs: pair_kernel(n_img, n_txt, width, *refs),
        out_shape=outs,
        in_specs=[VMEM] * (n_img + n_txt),
        out_specs=[VMEM] * len(outs),
        scratch_shapes=[pltpu.VMEM((n_img * rows, full), b16), pltpu.VMEM((n_txt * rows, full), b16)],
        name="pair",
    )(*images, *texts)


def fold_kernel(keep_ref, swap_ref, own_out, *outs):
    rows = own_out.shape[0]
    for k, out in enumerate((own_out, *outs)):
        at = slice(k * rows, (k + 1) * rows)
        out[...] = (keep_ref[at, :] + swap_ref[at, :].astype(jnp.float32)).astype(out.dtype)


def fold(keep, swap, rows):
    total, width = keep.shape
    outs = [jax.ShapeDtypeStruct((rows, width), jnp.float32)]
    outs += [jax.ShapeDtypeStruct((rows, width), jnp.bfloat16)] * (total // rows - 1)
    return pl.pallas_call(
        fold_kernel, out_shape=outs, in_specs=[VMEM] * 2, out_specs=[VMEM] * len(outs), name="fold",
    )(keep, swap)


def project_kernel(embed_ref, own_ref, *refs):
    *parts, out = refs
    values = embed_ref[...].astype(jnp.float32)
    inverse = lax.rsqrt(jnp.sum(values * values, axis=1, keepdims=True) + 1e-06)
    unit = values * inverse
    grad = own_ref[...]
    for part in parts:
        grad = grad + part[...].astype(jnp.float32)
    along = jnp.sum(unit * grad, axis=1, keepdims=True)
    out[...] = (grad - unit * along) * inverse


def project(embed, own, parts, name):
    return pl.pallas_call(
        project_kernel,
        out_shape=jax.ShapeDtypeStruct(own.shape, jnp.float32),
        in_specs=[VMEM] * (2 + len(parts)),
        out_specs=VMEM,
        name=name,
    )(embed, own, *parts)


def core_mask(mesh, axes):
    order = [mesh.axis_names.index(a) for a in mesh.axis_names if a not in axes] + [mesh.axis_names.index(a) for a in axes]
    n = 1
    for a in axes:
        n *= mesh.shape[a]
    devices = mesh.devices.transpose(order).reshape(-1, n)
    mask = 1
    while mask < n:
        same = all(
            getattr(row[i], "coords", None) is not None and row[i].coords == row[i ^ mask].coords
            for row in devices for i in range(n)
        )
        if same:
            return mask
        mask *= 2
    return 1


def solution(mesh):
    img_axes, txt_axes = "rep", ("blk", "sub")
    n_img = mesh.shape["rep"]
    n_txt = mesh.shape["blk"] * mesh.shape["sub"]
    swap = core_mask(mesh, txt_axes)
    near = [k for k in range(n_txt) if not k & swap]

    def move(array, axes, n, k):
        return lax.ppermute(array, axes, [(i, i ^ k) for i in range(n)])

    def body(image_embed, text_embed, image_ids, text_ids):
        rows, width = image_embed.shape
        img, txt = pack(image_embed, text_embed, image_ids, text_ids)
        images = [img] + [move(img, img_axes, n_img, k) for k in range(1, n_img)]
        texts = [txt] + [move(txt, txt_axes, n_txt, k) for k in near[1:]]
        texts += [move(t, txt_axes, n_txt, swap) for t in texts]
        *img_terms, keep, other = pair_terms(images, texts, width)
        img_parts = [move(img_terms[k], img_axes, n_img, k) for k in range(1, n_img)]
        other = move(other, txt_axes, n_txt, swap)
        txt_terms = fold(keep, other, rows)
        txt_parts = [move(t, txt_axes, n_txt, k) for t, k in zip(txt_terms[1:], near[1:])]
        return (
            project(image_embed, img_terms[0], img_parts, "project_image"),
            project(text_embed, txt_terms[0], txt_parts, "project_text"),
        )

    split = P(("blk", "rep", "sub"))
    return jax.shard_map(
        body,
        mesh=mesh,
        in_specs=(P(("blk", "rep", "sub"), None), P(("blk", "rep", "sub"), None), split, split),
        out_specs=(P(("blk", "rep", "sub"), None), P(("blk", "rep", "sub"), None)),
        check_vma=False,
    )
```
